32 devices in a mesh: sky: 2 (over x), vel: 16 (over z, y, core).
Axes of the slice: x: 2, y: 2, z: 4, core: 2. Of those that a mesh axis runs over, the one named last changes fastest.
Arguments:
- psi: bfloat16 [2, 512, 1024], P(None, 'vel', 'sky'), may hold values from -6 to 6
- phi: bfloat16 [2, 512, 1024], P(None, 'vel', 'sky'), may hold values from 0.25 to 4
- shifts: int32 [512, 2, 2], P('vel'), may hold values from -16 to 16, as said below
- tile_mask: int32 [2, 2], replicated, may hold values 0 or 1
Outputs:
- best: float32 [512, 1024], P('vel', 'sky')
The draws below stay inside these ranges and needn't reach their ends.
Inputs may be any that keep to these rules, and one draw needn't show every extreme that they name: `shifts`: pixel offsets of an epoch's image; entry 0 is a row offset, entry 1 a column offset.
All inputs are finite; a program needn't handle non-finite values.
Results may differ from the reference program's by a relative error of at most 0.0003.
Values may be sent and summed in bfloat16 or wider, within the bound.
No kernel may reach another device: no remote copies, remote signals or barrier semaphores. Data moves between devices by JAX's collectives and lax.ppermute only.
A program may use at most 64 MiB of HBM per device.

```python
import math
import jax
import jax.numpy as jnp
from jax import lax

TILE = 512
EPOCHS = 2
MAXS = 16
VELS = 512
FIELD_W = 1024
N_SKY = 2


def draw_shifts(key, part):
    values = jax.random.randint(key, (VELS, EPOCHS, 2), -MAXS, MAXS + 1)
    values = values.at[0, 0, 1].set(MAXS).at[1, 0, 1].set(-MAXS)
    values = values.at[2, 0, 0].set(MAXS).at[3, 0, 0].set(-MAXS)
    return values.astype(jnp.int32)


def touch_ends(values, own_key, low, top_value):
    extent = values.shape
    place = [jax.random.randint(jax.random.fold_in(own_key, axis), (), 0, extent[axis]) for axis in range(len(extent))]
    values = values.at[tuple(place)].set(low)
    longest = extent.index(max(extent))
    place[longest] = (place[longest] + 1) % extent[longest]
    return values.at[tuple(place)].set(top_value)


def shard_levels(rng, extent, split, least, top_value):
    gain, own = 1.0, jax.random.fold_in(rng, 6)
    for dim, shards_of in split:
        heights = jnp.exp(jax.random.uniform(jax.random.fold_in(own, dim), (shards_of,), jnp.float32, least / len(split), top_value / len(split)))
        gain = gain * jnp.repeat(heights, extent[dim] // shards_of).reshape([-1 if axis == dim else 1 for axis in range(len(extent))])
    return gain


def bell_draw(rng, dims, width, most, split=(), held_as=jnp.bfloat16):
    gain = shard_levels(rng, dims, split, -0.22, 0.18) if split else 1.0
    values = jax.random.normal(rng, dims, jnp.float32) * width * gain
    return jnp.minimum(jnp.maximum(values, -most), most).astype(held_as)


def setup_inputs(seed: int = 0) -> dict:
    arg_keys = jax.random.split(jax.random.key(seed), 5)
    return {
        "psi": bell_draw(arg_keys[0], (EPOCHS, TILE, FIELD_W), 1.0, 6.0, ((1, 16), (2, 2))),
        "phi": jnp.clip(jnp.exp(math.log(4.0) - 2.7725887 * jax.random.uniform(arg_keys[1], (EPOCHS, TILE, FIELD_W), jnp.float32) ** shard_levels(arg_keys[1], (EPOCHS, TILE, FIELD_W), ((1, 16), (2, 2)), -0.2, 0.2)), 0.25, 4.0).astype(jnp.bfloat16),
        "shifts": draw_shifts(jax.random.fold_in(arg_keys[4], 71), 0),
        "tile_mask": touch_ends((jax.random.randint(arg_keys[3], (EPOCHS, N_SKY), 0, 4) < 3).astype(jnp.int32), jax.random.fold_in(arg_keys[3], 1), 0, 1),
    }


def reference(psi, phi, shifts, tile_mask):
    keep = jnp.repeat(tile_mask.astype(jnp.bfloat16), TILE, axis=1)[:, None, :]
    stacked = jnp.stack([psi * keep, phi * keep])
    padded = jnp.pad(stacked, ((0, 0), (0, 0), (MAXS, MAXS), (MAXS, MAXS)))

    def advance(velocity, record):
        psi_total = jnp.zeros((TILE, FIELD_W), jnp.float32)
        phi_total = jnp.zeros((TILE, FIELD_W), jnp.float32)
        for epoch in range(EPOCHS):
            row_at = (MAXS + shifts[velocity, epoch, 0]).astype(jnp.int32)
            col_at = (MAXS + shifts[velocity, epoch, 1]).astype(jnp.int32)
            psi_total = psi_total + lax.dynamic_slice(padded[0, epoch], (row_at, col_at), (TILE, FIELD_W)).astype(jnp.float32)
            phi_total = phi_total + lax.dynamic_slice(padded[1, epoch], (row_at, col_at), (TILE, FIELD_W)).astype(jnp.float32)
        ratio_map = psi_total / jnp.sqrt(jnp.maximum(phi_total, 1.0))
        return jnp.maximum(record, ratio_map)
    start = jnp.full((TILE, FIELD_W), -1e+30, jnp.float32)
    return lax.fori_loop(0, VELS, advance, start)
```

```python
import functools

import jax
import jax.numpy as jnp
from jax import lax
from jax.experimental import pallas as pl
from jax.experimental.pallas import tpu as pltpu
from jax.sharding import PartitionSpec as P

MAXS = 16
LANES = 128
SUBLANES = 8


def search_kernel(pieces, n_sky, height, breadth, epochs, *refs):
    tables, refs = refs[:pieces], refs[pieces:]
    mask_ref, own_ref, above_ref, below_ref, left_ref, right_ref, best_ref, window, copies = refs
    spots = 2 * MAXS + 1
    rows = height + 2 * MAXS
    tiles = breadth // LANES
    sky = lax.axis_index("sky")

    for epoch in range(epochs):
        for image in range(2):
            at = (epoch, image)
            window[at + (slice(0, MAXS),)] = above_ref[at].astype(jnp.float32)
            window[at + (slice(MAXS + height, rows),)] = below_ref[at].astype(jnp.float32)
            mid = slice(MAXS, MAXS + height)
            window[at + (mid, slice(0, LANES))] = left_ref[at].astype(jnp.float32)
            window[at + (mid, slice(LANES, LANES + breadth))] = own_ref[at].astype(jnp.float32)
            window[at + (mid, slice(LANES + breadth, 2 * LANES + breadth))] = right_ref[at].astype(jnp.float32)

    lane = lax.broadcasted_iota(jnp.int32, (SUBLANES, LANES), 1)
    row_tiles = rows // SUBLANES

    def shift_columns(step, unused):
        epoch = step // (2 * row_tiles)
        image = (step // row_tiles) % 2
        row = pl.multiple_of((step % row_tiles) * SUBLANES, SUBLANES)
        found = []
        for tile in range(tiles + 2):
            at = sky + (0 if 0 < tile <= tiles else (-1 if tile == 0 else 1))
            inside = jnp.logical_and(at >= 0, at < n_sky)
            keep = jnp.where(inside, mask_ref[epoch, jnp.clip(at, 0, n_sky - 1)], 0).astype(jnp.float32)
            part = window[epoch, image, pl.ds(row, SUBLANES), tile * LANES:(tile + 1) * LANES]
            found.append(part * keep)
        for spot in range(spots):
            offset = spot - MAXS
            if offset == 0:
                outs = found[1:-1]
            elif offset > 0:
                turned = [pltpu.roll(part, LANES - offset, 1) for part in found[1:]]
                outs = [jnp.where(lane < LANES - offset, turned[t], turned[t + 1]) for t in range(tiles)]
            else:
                turned = [pltpu.roll(part, -offset, 1) for part in found[:-1]]
                outs = [jnp.where(lane >= -offset, turned[t + 1], turned[t]) for t in range(tiles)]
            for tile in range(tiles):
                slab = ((epoch * spots + spot) * 2 + image) * tiles + tile
                copies[pl.ds(pl.multiple_of(slab * rows + row, SUBLANES), SUBLANES), :] = outs[tile]
        return unused

    lax.fori_loop(0, epochs * 2 * row_tiles, shift_columns, 0)

    per_velocity = epochs * 2

    def velocity(table, index, group, best):
        bases = []
        for epoch in range(epochs):
            down = table[group, index * per_velocity + 2 * epoch]
            across = table[group, index * per_velocity + 2 * epoch + 1]
            bases.append((across + (MAXS + epoch * spots)) * (2 * tiles * rows) + down + MAXS)
        out = []
        for tile in range(tiles):
            psi_sum = sum(copies[pl.ds(base + tile * rows, height), :] for base in bases)
            phi_sum = sum(copies[pl.ds(base + (tiles + tile) * rows, height), :] for base in bases)
            out.append(jnp.maximum(best[tile], psi_sum * lax.rsqrt(jnp.maximum(phi_sum, 1.0))))
        return tuple(out)

    best = tuple(jnp.full((height, LANES), -1e30, jnp.float32) for _ in range(tiles))
    unroll = 4
    for table in tables:
        groups, width = table.shape
        count = width // per_velocity // unroll

        def steps(step, best):
            group, first = step // count, (step % count) * unroll
            for member in range(unroll):
                best = velocity(table, first + member, group, best)
            return best

        best = lax.fori_loop(0, groups * count, steps, best)
    for tile in range(tiles):
        best_ref[:, tile * LANES:(tile + 1) * LANES] = best[tile]


def gathered(piece, axis):
    count = lax.axis_size(axis)
    held, stride = piece, 1
    parts = [piece]
    while stride < count:
        radix = 4 if (count // stride) % 4 == 0 else 2
        if stride > 1:
            held = jnp.concatenate(parts, axis=0)
        parts = [held]
        for turn in range(1, radix):
            pairs = []
            for i in range(count):
                digit = (i // stride) % radix
                pairs.append((i, i + (((digit + turn) % radix) - digit) * stride))
            parts.append(lax.ppermute(held, axis, pairs))
        stride *= radix
    return parts


def body(psi, phi, shifts, tile_mask):
    epochs, height, breadth = psi.shape
    n_sky, n_vel = lax.axis_size("sky"), lax.axis_size("vel")
    own = jnp.stack([psi, phi], axis=1)
    sky_up = [(i, i + 1) for i in range(n_sky - 1)]
    sky_down = [(i + 1, i) for i in range(n_sky - 1)]
    left = lax.ppermute(own[..., breadth - LANES:], "sky", sky_up)
    right = lax.ppermute(own[..., :LANES], "sky", sky_down)
    tables = gathered(shifts.reshape(1, -1), "vel")
    wide = jnp.concatenate([left, own, right], axis=-1)
    vel_up = [(i, i + 1) for i in range(n_vel - 1)]
    vel_down = [(i + 1, i) for i in range(n_vel - 1)]
    above = lax.ppermute(wide[:, :, height - MAXS:], "vel", vel_up)
    below = lax.ppermute(wide[:, :, :MAXS], "vel", vel_down)
    vmem = pl.BlockSpec(memory_space=pltpu.VMEM)
    smem = pl.BlockSpec(memory_space=pltpu.SMEM)
    rows = height + 2 * MAXS
    slabs = epochs * (2 * MAXS + 1) * 2 * (breadth // LANES)
    return pl.pallas_call(
        functools.partial(search_kernel, len(tables), n_sky, height, breadth, epochs),
        out_shape=jax.ShapeDtypeStruct((height, breadth), jnp.float32),
        in_specs=[smem] * (len(tables) + 1) + [vmem] * 5,
        out_specs=vmem,
        scratch_shapes=[
            pltpu.VMEM((epochs, 2, rows, breadth + 2 * LANES), jnp.float32),
            pltpu.VMEM((slabs * rows, LANES), jnp.float32),
        ],
        compiler_params=pltpu.CompilerParams(vmem_limit_bytes=40 * 2**20),
        name="search",
    )(*tables, tile_mask, own, above, below, left, right)


def solution(mesh):
    placed = (P(None, "vel", "sky"), P(None, "vel", "sky"), P("vel", None, None), P())
    return jax.shard_map(
        body, mesh=mesh, in_specs=placed, out_specs=P("vel", "sky"), check_vma=False
    )
```

```python
import functools

import jax
import jax.numpy as jnp
from jax import lax
from jax.experimental import pallas as pl
from jax.experimental.pallas import tpu as pltpu
from jax.sharding import PartitionSpec as P

MAXS = 16
LANES = 128
SUBLANES = 8


def search_kernel(pieces, n_sky, height, breadth, epochs, *refs):
    tables, refs = refs[:pieces], refs[pieces:]
    mask_ref, own_ref, near_ref, far_ref, *side_refs, best_ref, pairs, copies = refs
    spots = 2 * MAXS + 1
    rows = height + 2 * MAXS
    tiles = breadth // LANES
    images = epochs * 2
    sky = lax.axis_index("sky")
    even = lax.rem(lax.axis_index("vel"), 2) == 0
    near_row = jnp.where(even, MAXS + height, 0)
    far_row = MAXS + height - near_row

    for epoch in range(epochs):
        keeps = []
        for step in (-1, 0, 1):
            at = sky + step
            inside = jnp.logical_and(at >= 0, at < n_sky)
            keep = mask_ref[epoch, jnp.clip(at, 0, n_sky - 1)]
            keeps.append(jnp.where(inside, keep, 0).astype(jnp.float32))
        for image in range(2):
            first = (epoch * 2 + image) * rows
            for tile in range(tiles + 2):
                keep = keeps[0 if tile == 0 else 2 if tile == tiles + 1 else 1]
                if 0 < tile <= tiles:
                    columns = slice((tile - 1) * LANES, tile * LANES)
                    middle = own_ref[epoch, image, :, columns]
                else:
                    side = 0 if tile == 0 else len(side_refs) - 1
                    columns = slice(breadth + side * LANES, breadth + (side + 1) * LANES)
                    middle = side_refs[side][epoch, image]
                parts = (
                    (near_row, MAXS, near_ref[epoch, image, :, columns]),
                    (MAXS, height, middle),
                    (far_row, MAXS, far_ref[epoch, image, :, columns]),
                )
                for row, count, part in parts:
                    part = (part.astype(jnp.float32) * keep).astype(jnp.bfloat16)
                    place = pl.ds(pl.multiple_of(first + row, MAXS), count)
                    if tile > 0:
                        pairs[tile - 1, place, LANES:] = part
                    if tile <= tiles:
                        pairs[tile, place, :LANES] = part

    ahead = lax.broadcasted_iota(jnp.int32, (2 * LANES, LANES), 0) - lax.broadcasted_iota(
        jnp.int32, (2 * LANES, LANES), 1
    )
    depth = images * rows

    def mover(distance):
        return jnp.where(ahead == distance, 1.0, 0.0).astype(jnp.bfloat16)

    def two_spots(source, spot, distance):
        units = jnp.concatenate([mover(distance), mover(distance + 1)], axis=1)
        moved = jnp.dot(
            pairs[source:source + tiles].reshape(tiles * depth, 2 * LANES), units, preferred_element_type=jnp.float32
        )
        for k in range(2):
            at = pl.multiple_of((spot + k) * (tiles * depth), SUBLANES)
            copies[pl.ds(at, tiles * depth), :] = moved[:, k * LANES:(k + 1) * LANES]

    def before(step, unused):
        two_spots(0, 2 * step, 2 * step + LANES - MAXS)
        return unused

    def after(step, unused):
        two_spots(1, 2 * step + 1 + MAXS, 2 * step + 1)
        return unused

    lax.fori_loop(0, MAXS // 2, before, 0, unroll=8)
    lax.fori_loop(0, MAXS // 2, after, 0, unroll=8)
    for tile in range(tiles):
        at = MAXS * tiles * depth + tile * depth
        copies[at:at + depth, :] = pairs[tile, :, LANES:].astype(jnp.float32)

    def velocity(table, first, best):
        bases = []
        for epoch in range(epochs):
            down, across = table[first + 2 * epoch], table[first + 2 * epoch + 1]
            bases.append((across + MAXS) * (tiles * depth) + down + (MAXS + epoch * 2 * rows))
        out = []
        for tile in range(tiles):
            psi_sum = sum(copies[pl.ds(base + tile * depth, height), :] for base in bases)
            phi_sum = sum(copies[pl.ds(base + (tile * depth + rows), height), :] for base in bases)
            out.append(jnp.maximum(best[tile], psi_sum * lax.rsqrt(jnp.maximum(phi_sum, 1.0))))
        return tuple(out)

    best = tuple(jnp.full((height, LANES), -1e30, jnp.float32) for _ in range(tiles))
    unroll, each = 4, epochs * 2
    for table in tables:

        def steps(step, best):
            for member in range(unroll):
                best = velocity(table, (step * unroll + member) * each, best)
            return best

        best = lax.fori_loop(0, table.shape[0] // (unroll * each), steps, best)
    for tile in range(tiles):
        best_ref[:, tile * LANES:(tile + 1) * LANES] = best[tile]


def gathered(piece, axis):
    count = lax.axis_size(axis)
    stride, parts = count, [piece]
    while stride > 1:
        radix = 4 if stride % 4 == 0 else 2
        stride //= radix
        held = jnp.concatenate(parts) if len(parts) > 1 else parts[0]
        parts = [held]
        for turn in range(1, radix):
            pairs = []
            for i in range(count):
                digit = (i // stride) % radix
                pairs.append((i, i + ((digit + turn) % radix - digit) * stride))
            parts.append(lax.ppermute(held, axis, pairs))
    return parts


def body(psi, phi, shifts, tile_mask):
    epochs, height, breadth = psi.shape
    n_sky, n_vel = lax.axis_size("sky"), lax.axis_size("vel")
    own = jnp.stack([psi, phi], axis=1)
    first, last = own[..., :LANES], own[..., breadth - LANES:]
    if n_sky == 2:
        edge = jnp.where(lax.axis_index("sky") == 0, last, first)
        sides = [lax.ppermute(edge, "sky", [(0, 1), (1, 0)])]
    else:
        sides = [
            lax.ppermute(last, "sky", [(i, i + 1) for i in range(n_sky - 1)]),
            lax.ppermute(first, "sky", [(i + 1, i) for i in range(n_sky - 1)]),
        ]
    tables = gathered(shifts.reshape(-1), "vel")
    wide = jnp.concatenate([own, *sides], axis=-1)
    even = lax.rem(lax.axis_index("vel"), 2) == 0
    top, bottom = wide[:, :, :MAXS], wide[:, :, height - MAXS:]
    near = lax.ppermute(jnp.where(even, bottom, top), "vel", [(i, i ^ 1) for i in range(n_vel)])
    others = [(i, ((i + 1) ^ 1) - 1) for i in range(1, n_vel - 1)]
    far = lax.ppermute(jnp.where(even, top, bottom), "vel", others)
    vmem = pl.BlockSpec(memory_space=pltpu.VMEM)
    smem = pl.BlockSpec(memory_space=pltpu.SMEM)
    rows = height + 2 * MAXS
    slabs = epochs * (2 * MAXS + 1) * 2 * (breadth // LANES)
    return pl.pallas_call(
        functools.partial(search_kernel, len(tables), n_sky, height, breadth, epochs),
        out_shape=jax.ShapeDtypeStruct((height, breadth), jnp.float32),
        in_specs=[smem] * (len(tables) + 1) + [vmem] * (3 + len(sides)),
        out_specs=vmem,
        scratch_shapes=[
            pltpu.VMEM((breadth // LANES + 1, epochs * 2 * rows, 2 * LANES), jnp.bfloat16),
            pltpu.VMEM((slabs * rows, LANES), jnp.float32),
        ],
        compiler_params=pltpu.CompilerParams(vmem_limit_bytes=40 * 2**20),
        name="search",
    )(*tables, tile_mask, own, near, far, *sides)


def solution(mesh):
    placed = (P(None, "vel", "sky"), P(None, "vel", "sky"), P("vel", None, None), P())
    return jax.shard_map(
        body, mesh=mesh, in_specs=placed, out_specs=P("vel", "sky"), check_vma=False
    )
```

```python
import functools
import operator

import jax
import jax.numpy as jnp
from jax import lax
from jax.experimental import pallas as pl
from jax.experimental.pallas import tpu as pltpu
from jax.sharding import PartitionSpec as P

MAXS = 16
LANES = 128
SUBLANES = 8


def search_kernel(pieces, n_sky, height, breadth, epochs, *refs):
    tables, refs = refs[:pieces], refs[pieces:]
    mask_ref, own_ref, near_ref, far_ref, *side_refs, best_ref, pairs, copies = refs
    spots = 2 * MAXS + 1
    rows = height + 2 * MAXS
    tiles = breadth // LANES
    images = epochs * 2
    sky = lax.axis_index("sky")
    even = lax.rem(lax.axis_index("vel"), 2) == 0
    near_row = jnp.where(even, MAXS + height, 0)
    far_row = MAXS + height - near_row

    for epoch in range(epochs):
        keeps = []
        for step in (-1, 0, 1):
            at = sky + step
            inside = jnp.logical_and(at >= 0, at < n_sky)
            keep = mask_ref[epoch, jnp.clip(at, 0, n_sky - 1)]
            keeps.append(jnp.where(inside, keep, 0).astype(jnp.float32))
        for image in range(2):
            first = (epoch * 2 + image) * rows
            for tile in range(tiles + 2):
                keep = keeps[0 if tile == 0 else 2 if tile == tiles + 1 else 1]
                if 0 < tile <= tiles:
                    columns = slice((tile - 1) * LANES, tile * LANES)
                    middle = own_ref[epoch, image, :, columns]
                else:
                    side = 0 if tile == 0 else len(side_refs) - 1
                    columns = slice(breadth + side * LANES, breadth + (side + 1) * LANES)
                    middle = side_refs[side][epoch, image]
                parts = (
                    (near_row, MAXS, near_ref[epoch, image, :, columns]),
                    (MAXS, height, middle),
                    (far_row, MAXS, far_ref[epoch, image, :, columns]),
                )
                for row, count, part in parts:
                    part = (part.astype(jnp.float32) * keep).astype(jnp.bfloat16)
                    place = pl.ds(pl.multiple_of(first + row, MAXS), count)
                    if tile > 0:
                        pairs[tile - 1, place, LANES:] = part
                    if tile <= tiles:
                        pairs[tile, place, :LANES] = part

    ahead = lax.broadcasted_iota(jnp.int32, (2 * LANES, LANES), 0) - lax.broadcasted_iota(
        jnp.int32, (2 * LANES, LANES), 1
    )
    depth = images * rows

    def mover(distance):
        return jnp.where(ahead == distance, 1.0, 0.0).astype(jnp.bfloat16)

    def two_spots(source, spot, distance):
        units = jnp.concatenate([mover(distance), mover(distance + 1)], axis=1)
        moved = jnp.dot(
            pairs[source:source + tiles].reshape(tiles * depth, 2 * LANES), units, preferred_element_type=jnp.float32
        )
        for k in range(2):
            at = pl.multiple_of((spot + k) * (tiles * depth), SUBLANES)
            copies[pl.ds(at, tiles * depth), :] = moved[:, k * LANES:(k + 1) * LANES]

    def before(step, unused):
        two_spots(0, 2 * step, 2 * step + LANES - MAXS)
        return unused

    def after(step, unused):
        two_spots(1, 2 * step + 1 + MAXS, 2 * step + 1)
        return unused

    lax.fori_loop(0, MAXS // 2, before, 0, unroll=8)
    lax.fori_loop(0, MAXS // 2, after, 0, unroll=8)
    for tile in range(tiles):
        at = MAXS * tiles * depth + tile * depth
        copies[at:at + depth, :] = pairs[tile, :, LANES:].astype(jnp.float32)

    def velocity(table, count, index, best):
        bases = []
        for epoch in range(epochs):
            down, across = table[2 * epoch * count + index], table[(2 * epoch + 1) * count + index]
            bases.append((across + MAXS) * (tiles * depth) + down + (MAXS + epoch * 2 * rows))
        out = []
        for part in range(len(best)):
            at = part // row_tiles * depth + part % row_tiles * SUBLANES
            psi_sum = functools.reduce(operator.add, [copies[pl.ds(base + at, SUBLANES), :] for base in bases])
            phi_sum = functools.reduce(operator.add, [copies[pl.ds(base + (at + rows), SUBLANES), :] for base in bases])
            out.append(jnp.maximum(best[part], psi_sum * lax.rsqrt(jnp.maximum(phi_sum, 1.0))))
        return tuple(out)

    row_tiles = height // SUBLANES
    best = tuple(jnp.full((SUBLANES, LANES), -1e30, jnp.float32) for _ in range(tiles * row_tiles))
    unroll = 4
    for table in tables:
        count = table.shape[0] // (2 * epochs)

        def steps(step, best):
            for member in range(unroll):
                best = velocity(table, count, step * unroll + member, best)
            return best

        best = lax.fori_loop(0, count // unroll, steps, best)
    for part in range(len(best)):
        tile, row = part // row_tiles, part % row_tiles * SUBLANES
        best_ref[row:row + SUBLANES, tile * LANES:(tile + 1) * LANES] = best[part]


def gathered(piece, axis):
    count = lax.axis_size(axis)
    stride, parts = count, [piece]
    while stride > 1:
        radix = 4 if stride % 4 == 0 else 2
        stride //= radix
        held = jnp.concatenate(parts, axis=-1) if len(parts) > 1 else piece
        parts = [held]
        for turn in range(radix - 1, 0, -1):
            pairs = [(i, i ^ (turn * stride)) for i in range(count)]
            parts.append(lax.ppermute(held, axis, pairs))
    return [jnp.concatenate([part.reshape(2 * part.shape[0], -1) for part in parts], axis=-1).reshape(-1)]


def body(psi, phi, shifts, tile_mask):
    epochs, height, breadth = psi.shape
    n_sky, n_vel = lax.axis_size("sky"), lax.axis_size("vel")
    own = jnp.stack([psi, phi], axis=1)
    first, last = own[..., :LANES], own[..., breadth - LANES:]
    if n_sky == 2:
        edge = jnp.where(lax.axis_index("sky") == 0, last, first)
        sides = [lax.ppermute(edge, "sky", [(0, 1), (1, 0)])]
    else:
        sides = [
            lax.ppermute(last, "sky", [(i, i + 1) for i in range(n_sky - 1)]),
            lax.ppermute(first, "sky", [(i + 1, i) for i in range(n_sky - 1)]),
        ]
    tables = gathered(jnp.transpose(shifts, (1, 2, 0)), "vel")
    wide = jnp.concatenate([own, *sides], axis=-1)
    even = lax.rem(lax.axis_index("vel"), 2) == 0
    top, bottom = wide[:, :, :MAXS], wide[:, :, height - MAXS:]
    near = lax.ppermute(jnp.where(even, bottom, top), "vel", [(i, i ^ 1) for i in range(n_vel)])
    others = [(i, ((i + 1) ^ 1) - 1) for i in range(1, n_vel - 1)]
    far = lax.ppermute(jnp.where(even, top, bottom), "vel", others)
    vmem = pl.BlockSpec(memory_space=pltpu.VMEM)
    smem = pl.BlockSpec(memory_space=pltpu.SMEM)
    rows = height + 2 * MAXS
    slabs = epochs * (2 * MAXS + 1) * 2 * (breadth // LANES)
    return pl.pallas_call(
        functools.partial(search_kernel, len(tables), n_sky, height, breadth, epochs),
        out_shape=jax.ShapeDtypeStruct((height, breadth), jnp.float32),
        in_specs=[smem] * (len(tables) + 1) + [vmem] * (3 + len(sides)),
        out_specs=vmem,
        scratch_shapes=[
            pltpu.VMEM((breadth // LANES + 1, epochs * 2 * rows, 2 * LANES), jnp.bfloat16),
            pltpu.VMEM((slabs * rows, LANES), jnp.float32),
        ],
        compiler_params=pltpu.CompilerParams(vmem_limit_bytes=40 * 2**20),
        name="search",
    )(*tables, tile_mask, own, near, far, *sides)


def solution(mesh):
    placed = (P(None, "vel", "sky"), P(None, "vel", "sky"), P("vel", None, None), P())
    return jax.shard_map(
        body, mesh=mesh, in_specs=placed, out_specs=P("vel", "sky"), check_vma=False
    )
```

```python
import functools
import operator

import jax
import jax.numpy as jnp
from jax import lax
from jax.experimental import pallas as pl
from jax.experimental.pallas import tpu as pltpu
from jax.sharding import PartitionSpec as P

MAXS = 16
LANES = 128
SUBLANES = 8


def search_kernel(n_sky, height, breadth, epochs, *refs):
    table, mask_ref, own_ref, near_ref, far_ref, *side_refs, best_ref, pairs, copies = refs
    spots = 2 * MAXS + 1
    rows = height + 2 * MAXS
    tiles = breadth // LANES
    images = epochs * 2
    sky = lax.axis_index("sky")
    even = lax.rem(lax.axis_index("vel"), 2) == 0
    near_row = jnp.where(even, MAXS + height, 0)
    far_row = MAXS + height - near_row

    for epoch in range(epochs):
        keeps = []
        for step in (-1, 0, 1):
            at = sky + step
            inside = jnp.logical_and(at >= 0, at < n_sky)
            keep = mask_ref[epoch, jnp.clip(at, 0, n_sky - 1)]
            keeps.append(jnp.where(inside, keep, 0).astype(jnp.float32))
        for image in range(2):
            first = (epoch * 2 + image) * rows
            for tile in range(tiles + 2):
                keep = keeps[0 if tile == 0 else 2 if tile == tiles + 1 else 1]
                if 0 < tile <= tiles:
                    columns = slice((tile - 1) * LANES, tile * LANES)
                    middle = own_ref[epoch, image, :, columns]
                else:
                    side = 0 if tile == 0 else len(side_refs) - 1
                    columns = slice(breadth + side * LANES, breadth + (side + 1) * LANES)
                    middle = side_refs[side][epoch, image]
                parts = (
                    (near_row, MAXS, near_ref[epoch, image, :, columns]),
                    (MAXS, height, middle),
                    (far_row, MAXS, far_ref[epoch, image, :, columns]),
                )
                for row, count, part in parts:
                    part = (part.astype(jnp.float32) * keep).astype(jnp.bfloat16)
                    place = pl.ds(pl.multiple_of(first + row, MAXS), count)
                    if tile > 0:
                        pairs[tile - 1, place, LANES:] = part
                    if tile <= tiles:
                        pairs[tile, place, :LANES] = part

    ahead = lax.broadcasted_iota(jnp.int32, (2 * LANES, LANES), 0) - lax.broadcasted_iota(
        jnp.int32, (2 * LANES, LANES), 1
    )
    depth = images * rows

    def mover(distance):
        return jnp.where(ahead == distance, 1.0, 0.0).astype(jnp.bfloat16)

    def two_spots(source, spot, distance):
        units = jnp.concatenate([mover(distance), mover(distance + 1)], axis=1)
        moved = jnp.dot(
            pairs[source:source + tiles].reshape(tiles * depth, 2 * LANES), units, preferred_element_type=jnp.float32
        )
        for k in range(2):
            at = pl.multiple_of((spot + k) * (tiles * depth), SUBLANES)
            copies[pl.ds(at, tiles * depth), :] = moved[:, k * LANES:(k + 1) * LANES]

    def before(step, unused):
        two_spots(0, 2 * step, 2 * step + LANES - MAXS)
        return unused

    def after(step, unused):
        two_spots(1, 2 * step + 1 + MAXS, 2 * step + 1)
        return unused

    lax.fori_loop(0, MAXS // 2, before, 0, unroll=8)
    lax.fori_loop(0, MAXS // 2, after, 0, unroll=8)
    for tile in range(tiles):
        at = MAXS * tiles * depth + tile * depth
        copies[at:at + depth, :] = pairs[tile, :, LANES:].astype(jnp.float32)

    def velocity(count, index, best):
        bases = []
        for epoch in range(epochs):
            down, across = table[2 * epoch * count + index], table[(2 * epoch + 1) * count + index]
            bases.append((across + MAXS) * (tiles * depth) + down + (MAXS + epoch * 2 * rows))
        out = []
        for part in range(len(best)):
            at = part // row_tiles * depth + part % row_tiles * SUBLANES
            psi_sum = functools.reduce(operator.add, [copies[pl.ds(base + at, SUBLANES), :] for base in bases])
            phi_sum = functools.reduce(operator.add, [copies[pl.ds(base + (at + rows), SUBLANES), :] for base in bases])
            out.append(jnp.maximum(best[part], psi_sum * lax.rsqrt(jnp.maximum(phi_sum, 1.0))))
        return tuple(out)

    row_tiles = height // SUBLANES
    best = tuple(jnp.full((SUBLANES, LANES), -1e30, jnp.float32) for _ in range(tiles * row_tiles))
    unroll = 4
    count = table.shape[0] // (2 * epochs)

    def steps(step, best):
        for member in range(unroll):
            best = velocity(count, step * unroll + member, best)
        return best

    best = lax.fori_loop(0, count // unroll, steps, best)
    for part in range(len(best)):
        tile, row = part // row_tiles, part % row_tiles * SUBLANES
        best_ref[row:row + SUBLANES, tile * LANES:(tile + 1) * LANES] = best[part]


def gathered(piece, axis):
    count = lax.axis_size(axis)
    stride, parts = 1, [piece]
    while stride < count:
        radix = 4 if count // stride % 4 == 0 else 2
        held = jnp.concatenate(parts, axis=-1) if len(parts) > 1 else piece
        parts = [held]
        for turn in range(radix - 1, 0, -1):
            parts.append(lax.ppermute(held, axis, [(i, i ^ (turn * stride)) for i in range(count)]))
        stride *= radix
    return jnp.concatenate(parts, axis=-1).reshape(-1)


def body(psi, phi, shifts, tile_mask):
    epochs, height, breadth = psi.shape
    n_sky, n_vel = lax.axis_size("sky"), lax.axis_size("vel")
    own = jnp.stack([psi, phi], axis=1)
    first, last = own[..., :LANES], own[..., breadth - LANES:]
    if n_sky == 2:
        edge = jnp.where(lax.axis_index("sky") == 0, last, first)
        sides = [lax.ppermute(edge, "sky", [(0, 1), (1, 0)])]
    else:
        sides = [
            lax.ppermute(last, "sky", [(i, i + 1) for i in range(n_sky - 1)]),
            lax.ppermute(first, "sky", [(i + 1, i) for i in range(n_sky - 1)]),
        ]
    table = gathered(jnp.transpose(shifts, (1, 2, 0)), "vel")
    wide = jnp.concatenate([own, *sides], axis=-1)
    even = lax.rem(lax.axis_index("vel"), 2) == 0
    top, bottom = wide[:, :, :MAXS], wide[:, :, height - MAXS:]
    near = lax.ppermute(jnp.where(even, bottom, top), "vel", [(i, i ^ 1) for i in range(n_vel)])
    others = [(i, ((i + 1) ^ 1) - 1) for i in range(1, n_vel - 1)]
    far = lax.ppermute(jnp.where(even, top, bottom), "vel", others)
    vmem = pl.BlockSpec(memory_space=pltpu.VMEM)
    smem = pl.BlockSpec(memory_space=pltpu.SMEM)
    rows = height + 2 * MAXS
    slabs = epochs * (2 * MAXS + 1) * 2 * (breadth // LANES)
    return pl.pallas_call(
        functools.partial(search_kernel, n_sky, height, breadth, epochs),
        out_shape=jax.ShapeDtypeStruct((height, breadth), jnp.float32),
        in_specs=[smem] * 2 + [vmem] * (3 + len(sides)),
        out_specs=vmem,
        scratch_shapes=[
            pltpu.VMEM((breadth // LANES + 1, epochs * 2 * rows, 2 * LANES), jnp.bfloat16),
            pltpu.VMEM((slabs * rows, LANES), jnp.float32),
        ],
        compiler_params=pltpu.CompilerParams(vmem_limit_bytes=40 * 2**20),
        name="search",
    )(table, tile_mask, own, near, far, *sides)


def solution(mesh):
    placed = (P(None, "vel", "sky"), P(None, "vel", "sky"), P("vel", None, None), P())
    return jax.shard_map(
        body, mesh=mesh, in_specs=placed, out_specs=P("vel", "sky"), check_vma=False
    )
```

```python
import functools
import operator

import jax
import jax.numpy as jnp
from jax import lax
from jax.experimental import pallas as pl
from jax.experimental.pallas import tpu as pltpu
from jax.sharding import PartitionSpec as P

MAXS = 16
LANES = 128
SUBLANES = 8


def search_kernel(n_sky, height, breadth, epochs, *refs):
    table_in, mask_ref, own_ref, near_ref, far_ref, *side_refs, best_ref, pairs, copies, table, arrived = refs
    table_copy = pltpu.make_async_copy(table_in, table, arrived)
    table_copy.start()
    spots = 2 * MAXS + 1
    rows = height + 2 * MAXS
    tiles = breadth // LANES
    images = epochs * 2
    sky = lax.axis_index("sky")
    even = lax.rem(lax.axis_index("vel"), 2) == 0
    near_row = jnp.where(even, MAXS + height, 0)
    far_row = MAXS + height - near_row

    for epoch in range(epochs):
        keeps = []
        for step in (-1, 0, 1):
            at = sky + step
            inside = jnp.logical_and(at >= 0, at < n_sky)
            keep = mask_ref[epoch, jnp.clip(at, 0, n_sky - 1)]
            keeps.append(jnp.where(inside, keep, 0).astype(jnp.float32))
        for image in range(2):
            first = (epoch * 2 + image) * rows
            for tile in range(tiles + 2):
                keep = keeps[0 if tile == 0 else 2 if tile == tiles + 1 else 1]
                if 0 < tile <= tiles:
                    columns = slice((tile - 1) * LANES, tile * LANES)
                    middle = own_ref[epoch, image, :, columns]
                else:
                    side = 0 if tile == 0 else len(side_refs) - 1
                    columns = slice(breadth + side * LANES, breadth + (side + 1) * LANES)
                    middle = side_refs[side][epoch, image]
                parts = (
                    (near_row, MAXS, near_ref[epoch, image, :, columns]),
                    (MAXS, height, middle),
                    (far_row, MAXS, far_ref[epoch, image, :, columns]),
                )
                for row, count, part in parts:
                    part = (part.astype(jnp.float32) * keep).astype(jnp.bfloat16)
                    place = pl.ds(pl.multiple_of(first + row, MAXS), count)
                    if tile > 0:
                        pairs[tile - 1, place, LANES:] = part
                    if tile <= tiles:
                        pairs[tile, place, :LANES] = part

    ahead = lax.broadcasted_iota(jnp.int32, (2 * LANES, LANES), 0) - lax.broadcasted_iota(
        jnp.int32, (2 * LANES, LANES), 1
    )
    depth = images * rows

    def mover(distance):
        return jnp.where(ahead == distance, 1.0, 0.0).astype(jnp.bfloat16)

    def two_spots(source, spot, distance):
        units = jnp.concatenate([mover(distance), mover(distance + 1)], axis=1)
        moved = jnp.dot(
            pairs[source:source + tiles].reshape(tiles * depth, 2 * LANES), units, preferred_element_type=jnp.float32
        )
        for k in range(2):
            at = pl.multiple_of((spot + k) * (tiles * depth), SUBLANES)
            copies[pl.ds(at, tiles * depth), :] = moved[:, k * LANES:(k + 1) * LANES]

    def before(step, unused):
        two_spots(0, 2 * step, 2 * step + LANES - MAXS)
        return unused

    def after(step, unused):
        two_spots(1, 2 * step + 1 + MAXS, 2 * step + 1)
        return unused

    lax.fori_loop(0, MAXS // 2, before, 0, unroll=8)
    lax.fori_loop(0, MAXS // 2, after, 0, unroll=8)
    for tile in range(tiles):
        at = MAXS * tiles * depth + tile * depth
        copies[at:at + depth, :] = pairs[tile, :, LANES:].astype(jnp.float32)

    def velocity(count, index, best):
        bases = []
        for epoch in range(epochs):
            down, across = table[2 * epoch * count + index], table[(2 * epoch + 1) * count + index]
            bases.append((across + MAXS) * (tiles * depth) + down + (MAXS + epoch * 2 * rows))
        out, waiting = list(best), []

        def finish():
            part, psi_sum, scale = waiting.pop(0)
            out[part] = jnp.maximum(out[part], psi_sum * scale)

        for part in range(len(best)):
            at = part // row_tiles * depth + part % row_tiles * SUBLANES
            psi_sum = functools.reduce(operator.add, [copies[pl.ds(base + at, SUBLANES), :] for base in bases])
            phi_sum = functools.reduce(operator.add, [copies[pl.ds(base + (at + rows), SUBLANES), :] for base in bases])
            waiting.append((part, psi_sum, lax.rsqrt(jnp.maximum(phi_sum, 1.0))))
            if len(waiting) > 3:
                finish()
        while waiting:
            finish()
        return tuple(out)

    row_tiles = height // SUBLANES
    best = tuple(jnp.full((SUBLANES, LANES), -1e30, jnp.float32) for _ in range(tiles * row_tiles))
    unroll = 4
    table_copy.wait()
    count = table.shape[0] // (2 * epochs)

    def steps(step, best):
        for member in range(unroll):
            best = velocity(count, step * unroll + member, best)
        return best

    best = lax.fori_loop(0, count // unroll, steps, best)
    for part in range(len(best)):
        tile, row = part // row_tiles, part % row_tiles * SUBLANES
        best_ref[row:row + SUBLANES, tile * LANES:(tile + 1) * LANES] = best[part]


def gathered(piece, axis):
    count = lax.axis_size(axis)
    stride, parts = 1, [piece]
    while stride < count:
        radix = 4 if count // stride % 4 == 0 else 2
        held = jnp.concatenate(parts, axis=-1) if len(parts) > 1 else piece
        parts = [held]
        for turn in range(radix - 1, 0, -1):
            parts.append(lax.ppermute(held, axis, [(i, i ^ (turn * stride)) for i in range(count)]))
        stride *= radix
    return jnp.concatenate(parts, axis=-1).reshape(-1)


def body(psi, phi, shifts, tile_mask):
    epochs, height, breadth = psi.shape
    n_sky, n_vel = lax.axis_size("sky"), lax.axis_size("vel")
    own = jnp.stack([psi, phi], axis=1)
    first, last = own[..., :LANES], own[..., breadth - LANES:]
    if n_sky == 2:
        edge = jnp.where(lax.axis_index("sky") == 0, last, first)
        sides = [lax.ppermute(edge, "sky", [(0, 1), (1, 0)])]
    else:
        sides = [
            lax.ppermute(last, "sky", [(i, i + 1) for i in range(n_sky - 1)]),
            lax.ppermute(first, "sky", [(i + 1, i) for i in range(n_sky - 1)]),
        ]
    table = gathered(jnp.transpose(shifts, (1, 2, 0)), "vel")
    wide = jnp.concatenate([own, *sides], axis=-1)
    even = lax.rem(lax.axis_index("vel"), 2) == 0
    top, bottom = wide[:, :, :MAXS], wide[:, :, height - MAXS:]
    near = lax.ppermute(jnp.where(even, bottom, top), "vel", [(i, i ^ 1) for i in range(n_vel)])
    others = [(i, ((i + 1) ^ 1) - 1) for i in range(1, n_vel - 1)]
    far = lax.ppermute(jnp.where(even, top, bottom), "vel", others)
    vmem = pl.BlockSpec(memory_space=pltpu.VMEM)
    smem = pl.BlockSpec(memory_space=pltpu.SMEM)
    rows = height + 2 * MAXS
    slabs = epochs * (2 * MAXS + 1) * 2 * (breadth // LANES)
    return pl.pallas_call(
        functools.partial(search_kernel, n_sky, height, breadth, epochs),
        out_shape=jax.ShapeDtypeStruct((height, breadth), jnp.float32),
        in_specs=[vmem, smem] + [vmem] * (3 + len(sides)),
        out_specs=vmem,
        scratch_shapes=[
            pltpu.VMEM((breadth // LANES + 1, epochs * 2 * rows, 2 * LANES), jnp.bfloat16),
            pltpu.VMEM((slabs * rows, LANES), jnp.float32),
            pltpu.SMEM(table.shape, jnp.int32),
            pltpu.SemaphoreType.DMA(()),
        ],
        compiler_params=pltpu.CompilerParams(vmem_limit_bytes=40 * 2**20),
        name="search",
    )(table, tile_mask, own, near, far, *sides)


def solution(mesh):
    placed = (P(None, "vel", "sky"), P(None, "vel", "sky"), P("vel", None, None), P())
    return jax.shard_map(
        body, mesh=mesh, in_specs=placed, out_specs=P("vel", "sky"), check_vma=False
    )
```

```python
import functools
import operator

import jax
import jax.numpy as jnp
from jax import lax
from jax.experimental import pallas as pl
from jax.experimental.pallas import tpu as pltpu
from jax.sharding import PartitionSpec as P

MAXS = 16
LANES = 128
SUBLANES = 8


def search_kernel(n_sky, height, breadth, epochs, *refs):
    table_in, mask_ref, own_ref, near_ref, far_ref, *side_refs, best_ref, pairs, copies, table, arrived = refs
    table_copy = pltpu.make_async_copy(table_in, table, arrived)
    table_copy.start()
    spots = 2 * MAXS + 1
    rows = height + 2 * MAXS
    tiles = breadth // LANES
    images = epochs * 2
    sky = lax.axis_index("sky")
    even = lax.rem(lax.axis_index("vel"), 2) == 0
    near_row = jnp.where(even, MAXS + height, 0)
    far_row = MAXS + height - near_row

    for epoch in range(epochs):
        keeps = []
        for step in (-1, 0, 1):
            at = sky + step
            inside = jnp.logical_and(at >= 0, at < n_sky)
            keep = mask_ref[epoch, jnp.clip(at, 0, n_sky - 1)]
            keeps.append(jnp.where(inside, keep, 0).astype(jnp.float32))
        for image in range(2):
            first = (epoch * 2 + image) * rows
            for tile in range(tiles + 2):
                keep = keeps[0 if tile == 0 else 2 if tile == tiles + 1 else 1]
                if 0 < tile <= tiles:
                    columns = slice((tile - 1) * LANES, tile * LANES)
                    middle = own_ref[epoch, image, :, columns]
                else:
                    side = 0 if tile == 0 else len(side_refs) - 1
                    columns = slice(breadth + side * LANES, breadth + (side + 1) * LANES)
                    middle = side_refs[side][epoch, image]
                parts = (
                    (near_row, MAXS, near_ref[epoch, image, :, columns]),
                    (MAXS, height, middle),
                    (far_row, MAXS, far_ref[epoch, image, :, columns]),
                )
                for row, count, part in parts:
                    part = (part.astype(jnp.float32) * keep).astype(jnp.bfloat16)
                    place = pl.ds(pl.multiple_of(first + row, MAXS), count)
                    if tile > 0:
                        pairs[tile - 1, place, LANES:] = part
                    if tile <= tiles:
                        pairs[tile, place, :LANES] = part

    ahead = lax.broadcasted_iota(jnp.int32, (2 * LANES, LANES), 0) - lax.broadcasted_iota(
        jnp.int32, (2 * LANES, LANES), 1
    )
    depth = images * rows

    def mover(distance):
        return jnp.where(ahead == distance, 1.0, 0.0).astype(jnp.bfloat16)

    def two_spots(source, spot, distance):
        units = jnp.concatenate([mover(distance), mover(distance + 1)], axis=1)
        moved = jnp.dot(
            pairs[source:source + tiles].reshape(tiles * depth, 2 * LANES), units, preferred_element_type=jnp.float32
        )
        for k in range(2):
            at = pl.multiple_of((spot + k) * (tiles * depth), SUBLANES)
            copies[pl.ds(at, tiles * depth), :] = moved[:, k * LANES:(k + 1) * LANES]

    def before(step, unused):
        two_spots(0, 2 * step, 2 * step + LANES - MAXS)
        return unused

    def after(step, unused):
        two_spots(1, 2 * step + 1 + MAXS, 2 * step + 1)
        return unused

    lax.fori_loop(0, MAXS // 2, before, 0, unroll=8)
    lax.fori_loop(0, MAXS // 2, after, 0, unroll=8)
    for tile in range(tiles):
        at = MAXS * tiles * depth + tile * depth
        copies[at:at + depth, :] = pairs[tile, :, LANES:].astype(jnp.float32)

    def velocity(count, index, best):
        bases = []
        for epoch in range(epochs):
            down, across = table[2 * epoch * count + index], table[(2 * epoch + 1) * count + index]
            bases.append((across + MAXS) * (tiles * depth) + down + (MAXS + epoch * 2 * rows))
        out, waiting = list(best), []

        def finish():
            part, psi_sum, scale = waiting.pop(0)
            out[part] = jnp.maximum(out[part], psi_sum * scale)

        for part in range(len(best)):
            at = part // row_tiles * depth + part % row_tiles * SUBLANES
            psi_sum = functools.reduce(operator.add, [copies[pl.ds(base + at, SUBLANES), :] for base in bases])
            phi_sum = functools.reduce(operator.add, [copies[pl.ds(base + (at + rows), SUBLANES), :] for base in bases])
            waiting.append((part, psi_sum, lax.rsqrt(jnp.maximum(phi_sum, 1.0))))
            if len(waiting) > 3:
                finish()
        while waiting:
            finish()
        return tuple(out)

    row_tiles = height // SUBLANES
    best = tuple(jnp.full((SUBLANES, LANES), -1e30, jnp.float32) for _ in range(tiles * row_tiles))
    unroll = 4
    table_copy.wait()
    count = table.shape[0] // (2 * epochs)

    def steps(step, best):
        for member in range(unroll):
            best = velocity(count, step * unroll + member, best)
        return best

    best = lax.fori_loop(0, count // unroll, steps, best)
    for part in range(len(best)):
        tile, row = part // row_tiles, part % row_tiles * SUBLANES
        best_ref[row:row + SUBLANES, tile * LANES:(tile + 1) * LANES] = best[part]


def gathered(piece, axis):
    count = lax.axis_size(axis)
    stride, parts = 1, [piece]
    while stride < count:
        radix = 4 if count // stride % 4 == 0 else 2
        held = jnp.concatenate(parts, axis=-1) if len(parts) > 1 else piece
        parts = [held]
        for turn in (3, 2, 1) if stride == 1 and radix == 4 else (2, 3, 1) if radix == 4 else (1,):
            parts.append(lax.ppermute(held, axis, [(i, i ^ (turn * stride)) for i in range(count)]))
        stride *= radix
    return jnp.concatenate(parts, axis=-1).reshape(-1)


def body(psi, phi, shifts, tile_mask):
    epochs, height, breadth = psi.shape
    n_sky, n_vel = lax.axis_size("sky"), lax.axis_size("vel")
    own = jnp.stack([psi, phi], axis=1)
    first, last = own[..., :LANES], own[..., breadth - LANES:]
    if n_sky == 2:
        edge = jnp.where(lax.axis_index("sky") == 0, last, first)
        sides = [lax.ppermute(edge, "sky", [(0, 1), (1, 0)])]
    else:
        sides = [
            lax.ppermute(last, "sky", [(i, i + 1) for i in range(n_sky - 1)]),
            lax.ppermute(first, "sky", [(i + 1, i) for i in range(n_sky - 1)]),
        ]
    table = gathered(jnp.transpose(shifts, (1, 2, 0)), "vel")
    wide = jnp.concatenate([own, *sides], axis=-1)
    even = lax.rem(lax.axis_index("vel"), 2) == 0
    top, bottom = wide[:, :, :MAXS], wide[:, :, height - MAXS:]
    near = lax.ppermute(jnp.where(even, bottom, top), "vel", [(i, i ^ 1) for i in range(n_vel)])
    others = [(i, ((i + 1) ^ 1) - 1) for i in range(1, n_vel - 1)]
    far = lax.ppermute(jnp.where(even, top, bottom), "vel", others)
    vmem = pl.BlockSpec(memory_space=pltpu.VMEM)
    smem = pl.BlockSpec(memory_space=pltpu.SMEM)
    rows = height + 2 * MAXS
    slabs = epochs * (2 * MAXS + 1) * 2 * (breadth // LANES)
    return pl.pallas_call(
        functools.partial(search_kernel, n_sky, height, breadth, epochs),
        out_shape=jax.ShapeDtypeStruct((height, breadth), jnp.float32),
        in_specs=[vmem, smem] + [vmem] * (3 + len(sides)),
        out_specs=vmem,
        scratch_shapes=[
            pltpu.VMEM((breadth // LANES + 1, epochs * 2 * rows, 2 * LANES), jnp.bfloat16),
            pltpu.VMEM((slabs * rows, LANES), jnp.float32),
            pltpu.SMEM(table.shape, jnp.int32),
            pltpu.SemaphoreType.DMA(()),
        ],
        compiler_params=pltpu.CompilerParams(vmem_limit_bytes=40 * 2**20),
        name="search",
    )(table, tile_mask, own, near, far, *sides)


def solution(mesh):
    placed = (P(None, "vel", "sky"), P(None, "vel", "sky"), P("vel", None, None), P())
    return jax.shard_map(
        body, mesh=mesh, in_specs=placed, out_specs=P("vel", "sky"), check_vma=False
    )
```
